32 devices in a mesh: leaf: 8 (over z, y), bond: 4 (over x, core).
Axes of the slice: x: 2, y: 2, z: 4, core: 2. Of those that a mesh axis runs over, the one named last changes fastest.
Arguments:
- leaf_metric: float32 [4, 32, 1024], P('bond', 'leaf'), may hold values from -257 to 257, as said below
- local_iso: float32 [24, 32, 1024], P('leaf', 'bond'), may hold values from -6 to 6
- top_iso: float32 [8, 32, 1024], P('leaf', 'bond'), may hold values from -6 to 6
Outputs:
- leaf_rho: float32 [4, 32, 1024], P('bond', 'leaf')
- inner_rho: float32 [4, 24, 1024], P('bond', 'leaf')
- top_rho: float32 [4, 8, 1024], P('bond', 'leaf')
The draws below stay inside these ranges and needn't reach their ends.
Inputs may be any that keep to these rules, and one draw needn't show every extreme that they name: Each entry of leaf_metric, taken as a 32 x 32 matrix, is symmetric positive definite.
All inputs are finite; a program needn't handle non-finite values.
Results may differ from the reference program's by a relative error of at most 0.0003.
Values sent between devices are 32-bit elements; how exact they have to be, the bound alone decides.
A program may use at most 64 MiB of HBM per device.

```python
import math
import jax
import jax.numpy as jnp
from jax import lax

CHI = 32
LEAVES_DEV = 4
CHI2 = 1024
LEAVES = 32
INNER = 24
BATCH = 4
N_LEAF = 8


def draw_leaf_metric(key, part):
    first_key, second_key = jax.random.split(key)
    base = jax.random.truncated_normal(first_key, -4.0, 4.0, (BATCH, LEAVES, CHI, CHI), jnp.float32)
    spread = jax.random.uniform(second_key, (BATCH, LEAVES, CHI), jnp.float32, math.log(0.4), math.log(2.5))
    rows = base * jnp.exp(spread)[..., None]
    metric = jnp.einsum('mlac,mlbc->mlab', rows, rows) / CHI + 0.5 * jnp.eye(CHI, dtype=jnp.float32)
    return metric.reshape(BATCH, LEAVES, CHI2)


def isometry_law(key, node_rows):
    keys = jax.random.split(key, 4)
    left_gain = jax.random.truncated_normal(keys[0], -4.0, 4.0, (node_rows, CHI), jnp.float32) / math.sqrt(CHI)
    right_gain = jax.random.truncated_normal(keys[1], -4.0, 4.0, (node_rows, CHI), jnp.float32) / math.sqrt(CHI)
    identity = jnp.eye(CHI, dtype=jnp.float32)
    structured = identity[None, :, :, None] * left_gain[:, None, None, :] + identity[None, :, None, :] * right_gain[:, None, :, None]
    noise = jax.random.truncated_normal(keys[2], -4.0, 4.0, (node_rows, CHI, CHI, CHI), jnp.float32) / CHI
    parent_scale = jnp.exp(jax.random.uniform(keys[3], (node_rows, CHI), jnp.float32, math.log(0.5), math.log(2.0)))
    return ((structured + noise) * parent_scale[:, :, None, None]).reshape(node_rows, CHI, CHI2)


def draw_local_iso(key, part):
    return isometry_law(jax.random.fold_in(key, 11), INNER)


def draw_top_iso(key, part):
    base_key = jax.random.fold_in(key, 23)
    levels = N_LEAF.bit_length() - 1
    blocks = []
    for height in range(1, levels + 1):
        groups = N_LEAF >> height
        logical = isometry_law(jax.random.fold_in(base_key, height), groups)
        width = CHI2 >> height
        shares = jnp.transpose(logical.reshape(groups, CHI, 2 ** height, width), (0, 2, 1, 3))
        blocks.append(shares.reshape(N_LEAF, CHI, width))
    root_tensor = isometry_law(jax.random.fold_in(base_key, 99), 1)
    width = CHI2 >> levels
    blocks.append(jnp.transpose(root_tensor.reshape(CHI, N_LEAF, width), (1, 0, 2)))
    return jnp.concatenate(blocks, axis=2)


def setup_inputs(seed: int = 0) -> dict:
    streams_of = jax.random.split(jax.random.key(seed), 4)
    return {
        "leaf_metric": draw_leaf_metric(jax.random.fold_in(streams_of[3], 71), 0),
        "local_iso": draw_local_iso(jax.random.fold_in(streams_of[3], 71), 0),
        "top_iso": draw_top_iso(jax.random.fold_in(streams_of[3], 71), 0),
    }


exact_mode = lax.Precision.HIGHEST


def normalize(matrix):
    trace_value = jnp.trace(matrix, axis1=-2, axis2=-1)
    return matrix * (CHI / trace_value)[..., None, None]


def grow(tensor, left_env, right_env):
    first = jnp.einsum('npab,mnac->mnpcb', tensor, left_env, precision=exact_mode)
    second = jnp.einsum('mnpcb,mnbd->mnpcd', first, right_env, precision=exact_mode)
    third = jnp.einsum('mnpcd,nqcd->mnpq', second, tensor, precision=exact_mode)
    return normalize(third)


def descend(tensor, parent_state, left_env, right_env):
    mixed = jnp.einsum('mnpq,npab->mnqab', parent_state, tensor, precision=exact_mode)
    left_part = jnp.einsum('mnqab,mnbd->mnqad', mixed, right_env, precision=exact_mode)
    left_state = jnp.einsum('mnqad,nqcd->mnac', left_part, tensor, precision=exact_mode)
    right_part = jnp.einsum('mnqab,mnac->mnqcb', mixed, left_env, precision=exact_mode)
    right_state = jnp.einsum('mnqcb,nqcd->mnbd', right_part, tensor, precision=exact_mode)
    return normalize(left_state), normalize(right_state)


def blockwise(function, tensor, *matrices):
    node_total = tensor.shape[0]
    per_block = min(node_total, 16)
    groups = node_total // per_block
    grouped_tensor = tensor.reshape((groups, per_block) + tensor.shape[1:])
    grouped = [jnp.moveaxis(item.reshape((item.shape[0], groups, per_block) + item.shape[2:]), 1, 0) for item in matrices]

    def apply_block(operands):
        return function(operands[0], *operands[1:])

    result = lax.map(apply_block, tuple([grouped_tensor] + grouped))

    def restore(item):
        moved = jnp.moveaxis(item, 0, 1)
        return moved.reshape((moved.shape[0], node_total) + moved.shape[3:])

    return jax.tree.map(restore, result)


def unpack_level(top_iso, height):
    width = CHI2 >> height
    start = CHI2 - (CHI2 >> (height - 1))
    block = top_iso[:, :, start:start + width]
    groups = N_LEAF >> height
    block = block.reshape(groups, 2 ** height, CHI, width)
    return jnp.transpose(block, (0, 2, 1, 3)).reshape(groups, CHI, CHI, CHI)


def unpack_root(top_iso, levels):
    width = CHI2 >> levels
    block = top_iso[:, :, CHI2 - width:]
    return jnp.transpose(block, (1, 0, 2)).reshape(CHI, CHI, CHI)


def reference(leaf_metric, local_iso, top_iso):
    levels_dev = LEAVES_DEV.bit_length() - 1
    top_levels = N_LEAF.bit_length() - 1
    leaves = leaf_metric.reshape(BATCH, LEAVES, CHI, CHI)
    local_all = local_iso.reshape(N_LEAF, LEAVES_DEV - 1, CHI, CHI, CHI)
    tensors = []
    for height in range(1, levels_dev + 1):
        node_count = LEAVES_DEV >> height
        offset = LEAVES_DEV - 2 * node_count
        tensors.append(local_all[:, offset:offset + node_count].reshape(-1, CHI, CHI, CHI))
    for height in range(1, top_levels + 1):
        tensors.append(unpack_level(top_iso, height))
    envs = [leaves]
    for tensor in tensors:
        current = envs[-1]
        envs.append(blockwise(grow, tensor, current[:, 0::2], current[:, 1::2]))
    root_env = envs[-1][:, 0]
    root_tensor = unpack_root(top_iso, top_levels)
    gram = jnp.einsum('pab,qab->pq', root_tensor, root_tensor, precision=exact_mode)
    state = jnp.broadcast_to(normalize(gram), (BATCH, 1, CHI, CHI))
    total = len(tensors)
    collected = [state] * (total + 1)
    for level_index in range(total - 1, -1, -1):
        children = envs[level_index]
        left_state, right_state = blockwise(descend, tensors[level_index], state, children[:, 0::2], children[:, 1::2])
        state = jnp.stack([left_state, right_state], axis=2).reshape(BATCH, -1, CHI, CHI)
        collected[level_index] = state
    top = jnp.zeros((BATCH, N_LEAF, CHI, CHI), jnp.float32)
    for height in range(1, top_levels + 1):
        top = top.at[:, 2 ** (height - 1) - 1::2 ** height].set(collected[levels_dev + height])
    top = top.at[:, N_LEAF - 1].set(root_env)
    inner = jnp.zeros((BATCH, N_LEAF, LEAVES_DEV - 1, CHI, CHI), jnp.float32)
    for height in range(1, levels_dev + 1):
        node_count = LEAVES_DEV >> height
        offset = LEAVES_DEV - 2 * node_count
        inner = inner.at[:, :, offset:offset + node_count].set(collected[height].reshape(BATCH, N_LEAF, node_count, CHI, CHI))
    leaf_rho = collected[0].reshape(BATCH, LEAVES, CHI2)
    inner_rho = inner.reshape(BATCH, INNER, CHI2)
    top_rho = top.reshape(BATCH, N_LEAF, CHI2)
    return (leaf_rho, inner_rho, top_rho)
```

```python
import functools

import jax
import jax.numpy as jnp
from jax import lax
from jax.experimental import pallas as pl
from jax.experimental.pallas import tpu as pltpu
from jax.sharding import PartitionSpec as P

LANES = 128
MESH = pl.DeviceIdType.MESH
EXACT = lax.Precision.HIGHEST


def mm(a, b):
    return jnp.dot(a, b, precision=EXACT, preferred_element_type=jnp.float32)


def mm_nt(a, b):
    return lax.dot_general(
        a, b, (((1,), (1,)), ((), ())), precision=EXACT, preferred_element_type=jnp.float32
    )


def kernel(
    cfg,
    leaf_ref,
    local_ref,
    top_ref,
    leaf_out,
    inner_out,
    top_out,
    raw,
    loc,
    wc,
    wrep,
    yt,
    fbuf,
    tbuf,
    esend,
    erecv,
    own_sem,
    loc_send,
    loc_recv,
    leaf_send,
    leaf_recv,
    fwd_send,
    fwd_recv,
    env_send,
    env_recv,
):
    chi, leaves, devices, bonds = cfg
    cols = chi * chi
    rep = LANES // chi
    chunks = cols // LANES
    levels = devices.bit_length() - 1
    height_dev = leaves.bit_length() - 1
    nodes = leaves - 1
    first = leaves // 2
    position = lax.axis_index("leaf")
    mine = lax.axis_index("bond")

    leaf_peers = [position ^ (1 << k) for k in range(levels)]
    bond_peers = [lax.rem(mine + r, bonds) for r in range(1, bonds)]

    barrier = pltpu.get_barrier_semaphore()
    for peer in leaf_peers:
        pl.semaphore_signal(barrier, inc=1, device_id=(peer, mine), device_id_type=MESH)
    for peer in bond_peers:
        pl.semaphore_signal(barrier, inc=1, device_id=(position, peer), device_id_type=MESH)
    own = [
        pltpu.make_async_copy(top_ref.at[0], raw.at[mine, position], own_sem.at[0]),
        pltpu.make_async_copy(local_ref, loc.at[mine], own_sem.at[1]),
    ]
    for copy in own:
        copy.start()
    pl.semaphore_wait(barrier, levels + bonds - 1)

    starts = [cols - (cols >> k) for k in range(levels + 1)]
    aligned = [s // LANES * LANES for s in starts]
    sends = []

    def local_copies(part, lo, hi):
        found = []
        for r, peer in enumerate(bond_peers):
            found.append(
                pltpu.make_async_remote_copy(
                    src_ref=local_ref.at[lo:hi],
                    dst_ref=loc.at[mine, lo:hi],
                    send_sem=loc_send.at[part, r],
                    recv_sem=loc_recv.at[part, r],
                    device_id=(position, peer),
                    device_id_type=MESH,
                )
            )
        for copy in found:
            copy.start()
        sends.extend(found)
        return found

    def leaf_copy(k):
        base = (position >> k) << k
        slots = raw.at[mine, pl.ds(base, 1 << k), :, aligned[k] : cols]
        source = slots if k else top_ref
        copy = pltpu.make_async_remote_copy(
            src_ref=source,
            dst_ref=slots,
            send_sem=leaf_send.at[k],
            recv_sem=leaf_recv.at[k],
            device_id=(leaf_peers[k], mine),
            device_id_type=MESH,
        )
        copy.start()
        sends.append(copy)
        return copy

    def forward_copies(k):
        base = (position >> (k + 1)) << (k + 1)
        stop = cols if k == levels - 1 else -(-starts[k + 1] // LANES) * LANES
        found = []
        for r, peer in enumerate(bond_peers):
            slots = raw.at[mine, pl.ds(base, 2 << k), :, aligned[k] : stop]
            found.append(
                pltpu.make_async_remote_copy(
                    src_ref=slots,
                    dst_ref=slots,
                    send_sem=fwd_send.at[k, r],
                    recv_sem=fwd_recv.at[k, r],
                    device_id=(position, peer),
                    device_id_type=MESH,
                )
            )
        for copy in found:
            copy.start()
        sends.extend(found)
        return found

    local_moves = [local_copies(0, 0, first)]
    leaf_moves = [leaf_copy(0)]
    if nodes > first:
        local_moves.append(local_copies(1, first, nodes))
    forward_moves = []
    for copy in own:
        copy.wait()

    def advance():
        k = len(forward_moves)
        if k < levels:
            leaf_moves[k].wait_recv()
            if k + 1 < levels:
                leaf_moves.append(leaf_copy(k + 1))
            forward_moves.append(forward_copies(k))

    row = lax.broadcasted_iota(jnp.int32, (chi, LANES), 0)
    lane = lax.broadcasted_iota(jnp.int32, (chi, LANES), 1)
    group = lane // chi
    row_mask = group == lax.rem(row, rep)
    diag_mask = row == lane
    big_row = lax.broadcasted_iota(jnp.int32, (LANES, LANES), 0)
    big_lane = lax.broadcasted_iota(jnp.int32, (LANES, LANES), 1)
    block_mask = big_row // chi == big_lane // chi
    pick = (
        lax.broadcasted_iota(jnp.int32, (chunks, chi), 1) // rep
        == lax.broadcasted_iota(jnp.int32, (chunks, chi), 0)
    ).astype(jnp.float32)
    spread = (
        lax.broadcasted_iota(jnp.int32, (chi, chunks), 0) // rep
        == lax.broadcasted_iota(jnp.int32, (chi, chunks), 1)
    ).astype(jnp.float32)
    widen = (
        lax.broadcasted_iota(jnp.int32, (chi, cols), 1) // chi
        == lax.broadcasted_iota(jnp.int32, (chi, cols), 0)
    ).astype(jnp.float32)

    def fold(value):
        shift = chi
        while shift < LANES:
            value = value + pltpu.roll(value, shift, 1)
            shift *= 2
        return value

    def normalize(matrix):
        trace = jnp.sum(jnp.where(diag_mask, matrix, 0.0), axis=(0, 1), keepdims=True)
        return matrix * (chi / trace)

    def unflatten(line):
        tile = jnp.concatenate(
            [line[:, g * LANES : (g + 1) * LANES] for g in range(chunks)], axis=0
        )
        return fold(jnp.where(row_mask, mm(spread, tile), 0.0))

    def flatten(matrix, out, index):
        tile = mm(pick, jnp.where(row_mask, matrix, 0.0))
        for g in range(chunks):
            out[0, index : index + 1, g * LANES : (g + 1) * LANES] = tile[g : g + 1]

    def lanes_to_rows(value):
        return jnp.concatenate(
            [value[:, g * LANES : (g + 1) * LANES] for g in range(chunks)], axis=0
        )

    def rows_to_lanes(value):
        return jnp.concatenate([value[g * chi : (g + 1) * chi] for g in range(chunks)], axis=1)

    def swap_children(value):
        for g in range(chunks):
            tbuf[g * LANES : (g + 1) * LANES, :] = value[:, g * LANES : (g + 1) * LANES].T
        pieces = []
        for g in range(chunks):
            block = jnp.concatenate(
                [tbuf[pl.ds(rep * g + i, chi, stride=chi), :] for i in range(rep)], axis=0
            )
            pieces.append(block.T)
        return jnp.concatenate(pieces, axis=1)

    def store(item, value):
        for g in range(chunks):
            chunk = value[:, g * LANES : (g + 1) * LANES]
            wc[item, g * chi : (g + 1) * chi, :] = chunk
            for i in range(rep):
                wrep[item, rep * g + i] = fold(jnp.where(group == i, chunk, 0.0))

    def act_minor(item, env):
        block = jnp.where(block_mask, jnp.concatenate([env] * rep, axis=0), 0.0)
        return rows_to_lanes(mm(wc[item], block))

    def act_major(item, env):
        fbuf[...] = mm(env[:, :chi], widen)

        def step(y, sums):
            line = fbuf[pl.ds(y, 1), :]
            block = wrep[item, y]
            return tuple(
                sums[g] + line[:, g * LANES : (g + 1) * LANES] * block for g in range(chunks)
            )

        zero = jnp.zeros((chi, LANES), jnp.float32)
        sums = lax.fori_loop(0, chi, step, (zero,) * chunks, unroll=4)
        yt[item] = jnp.concatenate(sums, axis=0).T
        return jnp.concatenate(sums, axis=1)

    def close(left, right):
        small = mm_nt(left, right)
        return normalize(jnp.concatenate([small] * rep, axis=1))

    def descend(item, state):
        mixed = mm(state[:, :chi], rows_to_lanes(wc[item]))
        square = jnp.where(block_mask, mm(yt[item], lanes_to_rows(mixed)), 0.0)
        total = square[:chi]
        for i in range(1, rep):
            total = total + square[i * chi : (i + 1) * chi]
        return normalize(fold(total))

    envs = [[unflatten(leaf_ref[0, n : n + 1, :]) for n in range(leaves)]]
    advance()
    for copy in local_moves[0]:
        copy.wait_recv()
    waited = 1
    node = 0
    for height in range(1, height_dev + 1):
        if height == 2:
            for copy in local_moves[1]:
                copy.wait_recv()
        current = envs[-1]
        grown = []
        for n in range(leaves >> height):
            value = jnp.concatenate([loc[j, node] for j in range(bonds)], axis=0)
            store(2 * node, value)
            store(2 * node + 1, swap_children(value))
            left, right = current[2 * n], current[2 * n + 1]
            by_left = act_major(2 * node, left)
            act_major(2 * node + 1, right)
            grown.append(close(act_minor(2 * node, right), by_left))
            node += 1
            advance()
        envs.append(grown)
    while len(forward_moves) < levels:
        advance()

    env = envs[-1][0]

    def assemble(k, start, width):
        count = min(2 << k, devices)
        base = (position >> (k + 1)) << (k + 1)
        rows = []
        for j in range(bonds):
            rows.append(
                jnp.concatenate(
                    [raw[j, base + s, :, start : start + width] for s in range(count)], axis=1
                )
            )
        return jnp.concatenate(rows, axis=0)

    exchanges = []
    for k in range(levels):
        esend[k] = env
        copy = pltpu.make_async_remote_copy(
            src_ref=esend.at[k],
            dst_ref=erecv.at[k],
            send_sem=env_send.at[k],
            recv_sem=env_recv.at[k],
            device_id=(leaf_peers[k], mine),
            device_id_type=MESH,
        )
        copy.start()
        sends.append(copy)
        for move in forward_moves[k]:
            move.wait_recv()
        item = 2 * nodes + k
        value = assemble(k, starts[k], cols >> (k + 1))
        upper = lax.rem(position >> k, 2) == 1
        store(item, jnp.where(upper, value, swap_children(value)))
        minor = act_minor(item, env)
        copy.wait_recv()
        env = close(minor, act_major(item, erecv[k]))

    root = assemble(levels - 1, starts[levels], cols >> levels)
    state = close(root, root)
    top = env
    for k in range(levels - 1, -1, -1):
        marked = lax.rem(position + 1, 2 << k) == 1 << k
        top = jnp.where(marked, state, top)
        state = descend(2 * nodes + k, state)
    flatten(top, top_out, 0)
    states = [state]
    for height in range(height_dev, 0, -1):
        count = leaves >> height
        offset = leaves - 2 * count
        below = []
        for n in range(count):
            node = offset + n
            flatten(states[n], inner_out, node)
            below.append(descend(2 * node + 1, states[n]))
            below.append(descend(2 * node, states[n]))
        states = below
    for n in range(leaves):
        flatten(states[n], leaf_out, n)
    for copy in sends:
        copy.wait_send()


def body(cfg, leaf_metric, local_iso, top_iso):
    chi, leaves, devices, bonds = cfg
    cols = chi * chi
    nodes = leaves - 1
    levels = devices.bit_length() - 1
    share = chi // bonds
    items = 2 * nodes + levels
    f32 = jnp.float32
    dma = pltpu.SemaphoreType.DMA
    vmem = pl.BlockSpec(memory_space=pltpu.VMEM)
    return pl.pallas_call(
        functools.partial(kernel, cfg),
        out_shape=(
            jax.ShapeDtypeStruct((1, leaves, cols), f32),
            jax.ShapeDtypeStruct((1, nodes, cols), f32),
            jax.ShapeDtypeStruct((1, 1, cols), f32),
        ),
        in_specs=[vmem] * 3,
        out_specs=(vmem,) * 3,
        scratch_shapes=[
            pltpu.VMEM((bonds, devices, share, cols), f32),
            pltpu.VMEM((bonds, nodes, share, cols), f32),
            pltpu.VMEM((items, cols * chi // LANES, LANES), f32),
            pltpu.VMEM((items, chi, chi, LANES), f32),
            pltpu.VMEM((items, LANES, cols * chi // LANES), f32),
            pltpu.VMEM((chi, cols), f32),
            pltpu.VMEM((cols, chi), f32),
            pltpu.VMEM((levels, chi, LANES), f32),
            pltpu.VMEM((levels, chi, LANES), f32),
            dma((2,)),
            dma((2, bonds - 1)),
            dma((2, bonds - 1)),
            dma((levels,)),
            dma((levels,)),
            dma((levels, bonds - 1)),
            dma((levels, bonds - 1)),
            dma((levels,)),
            dma((levels,)),
        ],
        compiler_params=pltpu.CompilerParams(collective_id=0, has_side_effects=True),
        name="tree_sweep",
    )(leaf_metric, local_iso, top_iso)


def solution(mesh):
    devices, bonds = mesh.shape["leaf"], mesh.shape["bond"]
    spec = P("bond", "leaf", None)
    iso = P("leaf", "bond", None)

    def whole(leaf_metric, local_iso, top_iso):
        cfg = (local_iso.shape[1], leaf_metric.shape[1] // devices, devices, bonds)
        return jax.shard_map(
            functools.partial(body, cfg),
            mesh=mesh,
            in_specs=(spec, iso, iso),
            out_specs=(spec, spec, spec),
            check_vma=False,
        )(leaf_metric, local_iso, top_iso)

    return whole
```

```python
import functools

import jax
import jax.numpy as jnp
from jax import lax
from jax.experimental import pallas as pl
from jax.experimental.pallas import tpu as pltpu
from jax.sharding import PartitionSpec as P

LANES = 128
MESH = pl.DeviceIdType.MESH
EXACT = lax.Precision.HIGHEST


def mm(a, b):
    return jnp.dot(a, b, precision=EXACT, preferred_element_type=jnp.float32)


def dot(a, b):
    return jnp.dot(a, b, preferred_element_type=jnp.float32)


def dot_nt(a, b):
    return lax.dot_general(a, b, (((1,), (1,)), ((), ())), preferred_element_type=jnp.float32)


def halves(value):
    high = value.astype(jnp.bfloat16)
    low = (value - high.astype(jnp.float32)).astype(jnp.bfloat16)
    return high, low


def join_lanes(value):
    return value[:, :LANES] + value[:, LANES:]


def join_rows(value):
    half = value.shape[0] // 2
    return value[:half] + value[half:]


def kernel(
    cfg,
    leaf_ref,
    local_ref,
    top_ref,
    leaf_out,
    inner_out,
    top_out,
    raw,
    loc,
    wk,
    wm,
    wrep,
    yt,
    fbuf,
    tbuf,
    esend,
    erecv,
    own_sem,
    loc_send,
    loc_recv,
    leaf_send,
    leaf_recv,
    fwd_send,
    fwd_recv,
    env_send,
    env_recv,
):
    chi, leaves, devices, bonds = cfg
    cols = chi * chi
    rep = LANES // chi
    chunks = cols // LANES
    levels = devices.bit_length() - 1
    height_dev = leaves.bit_length() - 1
    nodes = leaves - 1
    first = leaves // 2
    position = lax.axis_index("leaf")
    mine = lax.axis_index("bond")

    leaf_peers = [position ^ (1 << k) for k in range(levels)]
    bond_peers = [lax.rem(mine + r, bonds) for r in range(1, bonds)]

    barrier = pltpu.get_barrier_semaphore()
    for peer in leaf_peers:
        pl.semaphore_signal(barrier, inc=1, device_id=(peer, mine), device_id_type=MESH)
    for peer in bond_peers:
        pl.semaphore_signal(barrier, inc=1, device_id=(position, peer), device_id_type=MESH)
    own = [
        pltpu.make_async_copy(top_ref.at[0], raw.at[mine, position], own_sem.at[0]),
        pltpu.make_async_copy(local_ref, loc.at[mine], own_sem.at[1]),
    ]
    for copy in own:
        copy.start()
    pl.semaphore_wait(barrier, levels + bonds - 1)

    starts = [cols - (cols >> k) for k in range(levels + 1)]
    aligned = [s // LANES * LANES for s in starts]
    sends = []

    def local_copies(part, lo, hi):
        found = []
        for r, peer in enumerate(bond_peers):
            found.append(
                pltpu.make_async_remote_copy(
                    src_ref=local_ref.at[lo:hi],
                    dst_ref=loc.at[mine, lo:hi],
                    send_sem=loc_send.at[part, r],
                    recv_sem=loc_recv.at[part, r],
                    device_id=(position, peer),
                    device_id_type=MESH,
                )
            )
        for copy in found:
            copy.start()
        sends.extend(found)
        return found

    def leaf_copy(k):
        base = (position >> k) << k
        slots = raw.at[mine, pl.ds(base, 1 << k), :, aligned[k] : cols]
        source = slots if k else top_ref
        copy = pltpu.make_async_remote_copy(
            src_ref=source,
            dst_ref=slots,
            send_sem=leaf_send.at[k],
            recv_sem=leaf_recv.at[k],
            device_id=(leaf_peers[k], mine),
            device_id_type=MESH,
        )
        copy.start()
        sends.append(copy)
        return copy

    def forward_copies(k):
        base = (position >> (k + 1)) << (k + 1)
        stop = cols if k == levels - 1 else -(-starts[k + 1] // LANES) * LANES
        found = []
        for r, peer in enumerate(bond_peers):
            slots = raw.at[mine, pl.ds(base, 2 << k), :, aligned[k] : stop]
            found.append(
                pltpu.make_async_remote_copy(
                    src_ref=slots,
                    dst_ref=slots,
                    send_sem=fwd_send.at[k, r],
                    recv_sem=fwd_recv.at[k, r],
                    device_id=(position, peer),
                    device_id_type=MESH,
                )
            )
        for copy in found:
            copy.start()
        sends.extend(found)
        return found

    local_moves = [local_copies(0, 0, first)]
    leaf_moves = [leaf_copy(0)]
    if nodes > first:
        local_moves.append(local_copies(1, first, nodes))
    forward_moves = []
    for copy in own:
        copy.wait()

    def advance():
        k = len(forward_moves)
        if k < levels:
            leaf_moves[k].wait_recv()
            if k + 1 < levels:
                leaf_moves.append(leaf_copy(k + 1))
            forward_moves.append(forward_copies(k))

    row = lax.broadcasted_iota(jnp.int32, (chi, LANES), 0)
    lane = lax.broadcasted_iota(jnp.int32, (chi, LANES), 1)
    group = lane // chi
    row_mask = group == lax.rem(row, rep)
    diag_mask = row == lane
    big_row = lax.broadcasted_iota(jnp.int32, (LANES, LANES), 0)
    big_lane = lax.broadcasted_iota(jnp.int32, (LANES, LANES), 1)
    block_mask = big_row // chi == big_lane // chi
    pick = (
        lax.broadcasted_iota(jnp.int32, (chunks, chi), 1) // rep
        == lax.broadcasted_iota(jnp.int32, (chunks, chi), 0)
    ).astype(jnp.float32)
    spread = (
        lax.broadcasted_iota(jnp.int32, (chi, chunks), 0) // rep
        == lax.broadcasted_iota(jnp.int32, (chi, chunks), 1)
    ).astype(jnp.float32)
    widen = (
        lax.broadcasted_iota(jnp.int32, (LANES, cols), 1) // chi
        == lax.rem(lax.broadcasted_iota(jnp.int32, (LANES, cols), 0), chi)
    ).astype(jnp.float32).astype(jnp.bfloat16)
    copy_row = lax.broadcasted_iota(jnp.int32, (2 * LANES, rep * LANES), 0)
    copy_lane = lax.broadcasted_iota(jnp.int32, (2 * LANES, rep * LANES), 1)
    copies = jnp.where(
        (lax.rem(copy_row, LANES) // chi == copy_lane // LANES)
        & (lax.rem(copy_row, chi) == lax.rem(copy_lane, chi)),
        1.0,
        0.0,
    ).astype(jnp.bfloat16)

    def fold(value):
        shift = chi
        while shift < LANES:
            value = value + pltpu.roll(value, shift, 1)
            shift *= 2
        return value

    def normalize(matrix):
        trace = jnp.sum(jnp.where(diag_mask, matrix, 0.0), axis=(0, 1), keepdims=True)
        return matrix * (chi / trace)

    def unflatten(line):
        tile = jnp.concatenate(
            [line[:, g * LANES : (g + 1) * LANES] for g in range(chunks)], axis=0
        )
        return fold(jnp.where(row_mask, mm(spread, tile), 0.0))

    def flatten(matrix, out, index):
        tile = mm(pick, jnp.where(row_mask, matrix, 0.0))
        for g in range(chunks):
            out[0, index : index + 1, g * LANES : (g + 1) * LANES] = tile[g : g + 1]

    def lanes_to_rows(value):
        return jnp.concatenate(
            [value[:, g * LANES : (g + 1) * LANES] for g in range(chunks)], axis=0
        )

    def rows_to_lanes(value):
        return jnp.concatenate([value[g * chi : (g + 1) * chi] for g in range(chunks)], axis=1)

    def swap_children(value):
        for g in range(chunks):
            tbuf[g * LANES : (g + 1) * LANES, :] = value[:, g * LANES : (g + 1) * LANES].T
        pieces = []
        for g in range(chunks):
            block = jnp.concatenate(
                [tbuf[pl.ds(rep * g + i, chi, stride=chi), :] for i in range(rep)], axis=0
            )
            pieces.append(block.T)
        return jnp.concatenate(pieces, axis=1)

    def store(item, value):
        high, low = halves(value)
        wm[item] = jnp.concatenate([high, low] * (rep // 2), axis=0)
        stack = jnp.concatenate([lanes_to_rows(high), lanes_to_rows(low)], axis=1)
        wk[item] = stack
        spread_out = dot(stack, copies)
        for g in range(chunks):
            for i in range(rep):
                wrep[item, rep * g + i] = spread_out[
                    g * chi : (g + 1) * chi, i * LANES : (i + 1) * LANES
                ]

    def act_minor(item, env):
        block = jnp.where(block_mask, jnp.concatenate([env] * rep, axis=0), 0.0)
        pair = jnp.concatenate(halves(block), axis=1)
        return rows_to_lanes(join_lanes(dot(wk[item], jnp.concatenate([pair, pair], axis=0))))

    def act_major(item, env):
        high = env.astype(jnp.bfloat16).astype(jnp.float32)
        rest = env - high
        middle = rest.astype(jnp.bfloat16).astype(jnp.float32)
        low = jnp.where(group == 2, rest - middle, 0.0)
        parts = jnp.where(group == 0, high, jnp.where(group == 1, middle, low))
        fbuf[...] = dot(parts.astype(jnp.bfloat16), widen)

        def step(y, sums):
            line = fbuf[pl.ds(y, 1), :]
            block = wrep[item, y]
            return tuple(
                sums[g] + line[:, g * LANES : (g + 1) * LANES] * block for g in range(chunks)
            )

        zero = jnp.zeros((chi, LANES), jnp.float32)
        sums = lax.fori_loop(0, chi, step, (zero,) * chunks, unroll=4)
        yt[item] = jnp.concatenate(halves(jnp.concatenate(sums, axis=0).T), axis=0)
        return jnp.concatenate(sums, axis=1)

    def close(left, right):
        high, low = halves(right)
        wide = jnp.concatenate([high] * rep + [low] * rep, axis=0)
        tall = jnp.concatenate(halves(left), axis=0)
        return normalize(join_lanes(join_rows(dot_nt(tall, wide))))

    def descend(item, state):
        high = state.astype(jnp.bfloat16).astype(jnp.float32)
        parts = jnp.where(group < rep // 2, high, state - high).astype(jnp.bfloat16)
        mixed = lanes_to_rows(dot(parts, wm[item]))
        square = dot(yt[item], jnp.concatenate(halves(mixed), axis=1))
        square = jnp.where(block_mask, join_lanes(join_rows(square)), 0.0)
        total = square[:chi]
        for i in range(1, rep):
            total = total + square[i * chi : (i + 1) * chi]
        return normalize(fold(total))

    envs = [[unflatten(leaf_ref[0, n : n + 1, :]) for n in range(leaves)]]
    advance()
    for copy in local_moves[0]:
        copy.wait_recv()
    waited = 1
    node = 0
    for height in range(1, height_dev + 1):
        if height == 2:
            for copy in local_moves[1]:
                copy.wait_recv()
        current = envs[-1]
        grown = []
        for n in range(leaves >> height):
            value = jnp.concatenate([loc[j, node] for j in range(bonds)], axis=0)
            store(2 * node, value)
            store(2 * node + 1, swap_children(value))
            left, right = current[2 * n], current[2 * n + 1]
            by_left = act_major(2 * node, left)
            act_major(2 * node + 1, right)
            grown.append(close(by_left, act_minor(2 * node, right)))
            node += 1
            advance()
        envs.append(grown)
    while len(forward_moves) < levels:
        advance()

    env = envs[-1][0]

    def assemble(k, start, width):
        count = min(2 << k, devices)
        base = (position >> (k + 1)) << (k + 1)
        rows = []
        for j in range(bonds):
            rows.append(
                jnp.concatenate(
                    [raw[j, base + s, :, start : start + width] for s in range(count)], axis=1
                )
            )
        return jnp.concatenate(rows, axis=0)

    exchanges = []
    for k in range(levels):
        esend[k] = env
        copy = pltpu.make_async_remote_copy(
            src_ref=esend.at[k],
            dst_ref=erecv.at[k],
            send_sem=env_send.at[k],
            recv_sem=env_recv.at[k],
            device_id=(leaf_peers[k], mine),
            device_id_type=MESH,
        )
        copy.start()
        sends.append(copy)
        for move in forward_moves[k]:
            move.wait_recv()
        item = 2 * nodes + k
        value = assemble(k, starts[k], cols >> (k + 1))
        upper = lax.rem(position >> k, 2) == 1
        store(item, jnp.where(upper, value, swap_children(value)))
        minor = act_minor(item, env)
        copy.wait_recv()
        env = close(act_major(item, erecv[k]), minor)

    root = assemble(levels - 1, starts[levels], cols >> levels)
    state = close(root, root)
    top = env
    for k in range(levels - 1, -1, -1):
        marked = lax.rem(position + 1, 2 << k) == 1 << k
        top = jnp.where(marked, state, top)
        state = descend(2 * nodes + k, state)
    flatten(top, top_out, 0)
    states = [state]
    for height in range(height_dev, 0, -1):
        count = leaves >> height
        offset = leaves - 2 * count
        below = []
        for n in range(count):
            node = offset + n
            flatten(states[n], inner_out, node)
            below.append(descend(2 * node + 1, states[n]))
            below.append(descend(2 * node, states[n]))
        states = below
    for n in range(leaves):
        flatten(states[n], leaf_out, n)
    for copy in sends:
        copy.wait_send()


def body(cfg, leaf_metric, local_iso, top_iso):
    chi, leaves, devices, bonds = cfg
    cols = chi * chi
    nodes = leaves - 1
    levels = devices.bit_length() - 1
    share = chi // bonds
    items = 2 * nodes + levels
    f32 = jnp.float32
    dma = pltpu.SemaphoreType.DMA
    vmem = pl.BlockSpec(memory_space=pltpu.VMEM)
    return pl.pallas_call(
        functools.partial(kernel, cfg),
        out_shape=(
            jax.ShapeDtypeStruct((1, leaves, cols), f32),
            jax.ShapeDtypeStruct((1, nodes, cols), f32),
            jax.ShapeDtypeStruct((1, 1, cols), f32),
        ),
        in_specs=[vmem] * 3,
        out_specs=(vmem,) * 3,
        scratch_shapes=[
            pltpu.VMEM((bonds, devices, share, cols), f32),
            pltpu.VMEM((bonds, nodes, share, cols), f32),
            pltpu.VMEM((items, cols * chi // LANES, 2 * LANES), jnp.bfloat16),
            pltpu.VMEM((items, LANES, cols), jnp.bfloat16),
            pltpu.VMEM((items, chi, chi, LANES), f32),
            pltpu.VMEM((items, 2 * LANES, cols * chi // LANES), jnp.bfloat16),
            pltpu.VMEM((chi, cols), f32),
            pltpu.VMEM((cols, chi), f32),
            pltpu.VMEM((levels, chi, LANES), f32),
            pltpu.VMEM((levels, chi, LANES), f32),
            dma((2,)),
            dma((2, bonds - 1)),
            dma((2, bonds - 1)),
            dma((levels,)),
            dma((levels,)),
            dma((levels, bonds - 1)),
            dma((levels, bonds - 1)),
            dma((levels,)),
            dma((levels,)),
        ],
        compiler_params=pltpu.CompilerParams(collective_id=0, has_side_effects=True),
        name="tree_sweep",
    )(leaf_metric, local_iso, top_iso)


def solution(mesh):
    devices, bonds = mesh.shape["leaf"], mesh.shape["bond"]
    spec = P("bond", "leaf", None)
    iso = P("leaf", "bond", None)

    def whole(leaf_metric, local_iso, top_iso):
        cfg = (local_iso.shape[1], leaf_metric.shape[1] // devices, devices, bonds)
        return jax.shard_map(
            functools.partial(body, cfg),
            mesh=mesh,
            in_specs=(spec, iso, iso),
            out_specs=(spec, spec, spec),
            check_vma=False,
        )(leaf_metric, local_iso, top_iso)

    return whole
```

```python
import functools

import jax
import jax.numpy as jnp
from jax import lax
from jax.experimental import pallas as pl
from jax.experimental.pallas import tpu as pltpu
from jax.sharding import PartitionSpec as P

LANES = 128
MESH = pl.DeviceIdType.MESH
EXACT = lax.Precision.HIGHEST


def mm(a, b):
    return jnp.dot(a, b, precision=EXACT, preferred_element_type=jnp.float32)


def dot(a, b):
    return jnp.dot(a, b, preferred_element_type=jnp.float32)


def dot_nt(a, b):
    return lax.dot_general(a, b, (((1,), (1,)), ((), ())), preferred_element_type=jnp.float32)


def halves(value):
    high = value.astype(jnp.bfloat16)
    low = (value - high.astype(jnp.float32)).astype(jnp.bfloat16)
    return high, low


def join_lanes(value):
    return value[:, :LANES] + value[:, LANES:]


def join_rows(value):
    half = value.shape[0] // 2
    return value[:half] + value[half:]


def kernel(
    cfg,
    leaf_ref,
    local_ref,
    top_ref,
    leaf_out,
    inner_out,
    top_out,
    raw,
    loc,
    wk,
    wm,
    wq,
    yt,
    fbuf,
    tbuf,
    esend,
    erecv,
    own_sem,
    loc_send,
    loc_recv,
    leaf_send,
    leaf_recv,
    fwd_send,
    fwd_recv,
    env_send,
    env_recv,
):
    chi, leaves, devices, bonds = cfg
    cols = chi * chi
    rep = LANES // chi
    chunks = cols // LANES
    levels = devices.bit_length() - 1
    height_dev = leaves.bit_length() - 1
    nodes = leaves - 1
    first = leaves // 2
    position = lax.axis_index("leaf")
    mine = lax.axis_index("bond")

    leaf_peers = [position ^ (1 << k) for k in range(levels)]
    bond_peers = [lax.rem(mine + r, bonds) for r in range(1, bonds)]

    barrier = pltpu.get_barrier_semaphore()
    for peer in leaf_peers:
        pl.semaphore_signal(barrier, inc=1, device_id=(peer, mine), device_id_type=MESH)
    for peer in bond_peers:
        pl.semaphore_signal(barrier, inc=1, device_id=(position, peer), device_id_type=MESH)
    own = [
        pltpu.make_async_copy(top_ref.at[0], raw.at[mine, position], own_sem.at[0]),
        pltpu.make_async_copy(local_ref, loc.at[mine], own_sem.at[1]),
    ]
    for copy in own:
        copy.start()
    pl.semaphore_wait(barrier, levels + bonds - 1)

    starts = [cols - (cols >> k) for k in range(levels + 1)]
    aligned = [s // LANES * LANES for s in starts]
    sends = []

    def local_copies(part, lo, hi):
        found = []
        for r, peer in enumerate(bond_peers):
            found.append(
                pltpu.make_async_remote_copy(
                    src_ref=local_ref.at[lo:hi],
                    dst_ref=loc.at[mine, lo:hi],
                    send_sem=loc_send.at[part, r],
                    recv_sem=loc_recv.at[part, r],
                    device_id=(position, peer),
                    device_id_type=MESH,
                )
            )
        for copy in found:
            copy.start()
        sends.extend(found)
        return found

    def leaf_copy(k):
        base = (position >> k) << k
        slots = raw.at[mine, pl.ds(base, 1 << k), :, aligned[k] : cols]
        source = slots if k else top_ref
        copy = pltpu.make_async_remote_copy(
            src_ref=source,
            dst_ref=slots,
            send_sem=leaf_send.at[k],
            recv_sem=leaf_recv.at[k],
            device_id=(leaf_peers[k], mine),
            device_id_type=MESH,
        )
        copy.start()
        sends.append(copy)
        return copy

    def forward_copies(k):
        base = (position >> (k + 1)) << (k + 1)
        stop = cols if k == levels - 1 else -(-starts[k + 1] // LANES) * LANES
        found = []
        for r, peer in enumerate(bond_peers):
            slots = raw.at[mine, pl.ds(base, 2 << k), :, aligned[k] : stop]
            found.append(
                pltpu.make_async_remote_copy(
                    src_ref=slots,
                    dst_ref=slots,
                    send_sem=fwd_send.at[k, r],
                    recv_sem=fwd_recv.at[k, r],
                    device_id=(position, peer),
                    device_id_type=MESH,
                )
            )
        for copy in found:
            copy.start()
        sends.extend(found)
        return found

    local_moves = [local_copies(0, 0, first)]
    leaf_moves = [leaf_copy(0)]
    if nodes > first:
        local_moves.append(local_copies(1, first, nodes))
    forward_moves = []
    for copy in own:
        copy.wait()

    def advance():
        k = len(forward_moves)
        if k < levels:
            leaf_moves[k].wait_recv()
            if k + 1 < levels:
                leaf_moves.append(leaf_copy(k + 1))
            forward_moves.append(forward_copies(k))

    row = lax.broadcasted_iota(jnp.int32, (chi, LANES), 0)
    lane = lax.broadcasted_iota(jnp.int32, (chi, LANES), 1)
    group = lane // chi
    row_mask = group == lax.rem(row, rep)
    diag_mask = row == lane
    big_row = lax.broadcasted_iota(jnp.int32, (LANES, LANES), 0)
    big_lane = lax.broadcasted_iota(jnp.int32, (LANES, LANES), 1)
    block_mask = big_row // chi == big_lane // chi
    pick = (
        lax.broadcasted_iota(jnp.int32, (chunks, chi), 1) // rep
        == lax.broadcasted_iota(jnp.int32, (chunks, chi), 0)
    ).astype(jnp.float32)
    spread = (
        lax.broadcasted_iota(jnp.int32, (chi, chunks), 0) // rep
        == lax.broadcasted_iota(jnp.int32, (chi, chunks), 1)
    ).astype(jnp.float32)
    sub = chi // rep
    widen = (
        lax.broadcasted_iota(jnp.int32, (LANES, chi * sub), 1) // sub
        == lax.rem(lax.broadcasted_iota(jnp.int32, (LANES, chi * sub), 0), chi)
    ).astype(jnp.float32).astype(jnp.bfloat16)
    unit_mask = lax.rem(
        lax.broadcasted_iota(jnp.int32, (sub, chi * sub), 1), sub
    ) == lax.broadcasted_iota(jnp.int32, (sub, chi * sub), 0)
    part_group = lax.broadcasted_iota(jnp.int32, (chunks * sub, LANES), 1) // chi

    def swap_groups(value):
        parts = [
            jnp.concatenate(
                [value[g * chi + v * sub : g * chi + (v + 1) * sub] for g in range(chunks)], axis=0
            )
            for v in range(rep)
        ]
        bit = 1
        while bit < rep:
            lower = lax.rem(part_group // bit, 2) == 0
            for a in range(rep):
                if a & bit == 0:
                    one, two = parts[a], parts[a | bit]
                    parts[a] = jnp.where(lower, one, pltpu.roll(two, bit * chi, 1))
                    parts[a | bit] = jnp.where(lower, pltpu.roll(one, LANES - bit * chi, 1), two)
            bit *= 2
        return jnp.concatenate(
            [parts[v][g * sub : (g + 1) * sub] for g in range(chunks) for v in range(rep)], axis=0
        )

    def fold(value):
        shift = chi
        while shift < LANES:
            value = value + pltpu.roll(value, shift, 1)
            shift *= 2
        return value

    def normalize(matrix):
        trace = jnp.sum(jnp.where(diag_mask, matrix, 0.0), axis=(0, 1), keepdims=True)
        return matrix * (chi / trace)

    def unflatten(line):
        tile = jnp.concatenate(
            [line[:, g * LANES : (g + 1) * LANES] for g in range(chunks)], axis=0
        )
        return fold(jnp.where(row_mask, mm(spread, tile), 0.0))

    def flatten(matrix, out, index):
        tile = mm(pick, jnp.where(row_mask, matrix, 0.0))
        for g in range(chunks):
            out[0, index : index + 1, g * LANES : (g + 1) * LANES] = tile[g : g + 1]

    def lanes_to_rows(value):
        return jnp.concatenate(
            [value[:, g * LANES : (g + 1) * LANES] for g in range(chunks)], axis=0
        )

    def rows_to_lanes(value):
        return jnp.concatenate([value[g * chi : (g + 1) * chi] for g in range(chunks)], axis=1)

    def swap_children(value):
        for g in range(chunks):
            tbuf[g * LANES : (g + 1) * LANES, :] = value[:, g * LANES : (g + 1) * LANES].T
        pieces = []
        for g in range(chunks):
            block = jnp.concatenate(
                [tbuf[pl.ds(rep * g + i, chi, stride=chi), :] for i in range(rep)], axis=0
            )
            pieces.append(block.T)
        return jnp.concatenate(pieces, axis=1)

    def store(item, value):
        high, low = halves(value)
        wm[item] = jnp.concatenate([high, low] * (rep // 2), axis=0)
        stack = jnp.concatenate([lanes_to_rows(high), lanes_to_rows(low)], axis=1)
        wk[item] = stack
        wq[item] = jnp.concatenate(halves(swap_groups(lanes_to_rows(value))), axis=1)

    def act_minor(item, env):
        block = jnp.where(block_mask, jnp.concatenate([env] * rep, axis=0), 0.0)
        pair = jnp.concatenate(halves(block), axis=1)
        return rows_to_lanes(join_lanes(dot(wk[item], jnp.concatenate([pair, pair], axis=0))))

    def act_major(item, env):
        high = env.astype(jnp.bfloat16).astype(jnp.float32)
        rest = env - high
        middle = rest.astype(jnp.bfloat16).astype(jnp.float32)
        low = jnp.where(group == 2, rest - middle, 0.0)
        parts = jnp.where(group == 0, high, jnp.where(group == 1, middle, low))
        fbuf[...] = dot(parts.astype(jnp.bfloat16), widen)
        wide = jnp.concatenate(
            [
                jnp.where(unit_mask, jnp.broadcast_to(fbuf[y : y + 1, :], unit_mask.shape), 0.0)
                for y in range(chi)
            ],
            axis=0,
        )
        acted = dot(jnp.concatenate(halves(wide), axis=0), wq[item])
        acted = swap_groups(join_lanes(join_rows(acted)))
        yt[item] = jnp.concatenate(halves(acted.T), axis=0)
        return rows_to_lanes(acted)

    def close(left, right):
        high, low = halves(right)
        wide = jnp.concatenate([high] * rep + [low] * rep, axis=0)
        tall = jnp.concatenate(halves(left), axis=0)
        return normalize(join_lanes(join_rows(dot_nt(tall, wide))))

    def descend(item, state):
        high = state.astype(jnp.bfloat16).astype(jnp.float32)
        parts = jnp.where(group < rep // 2, high, state - high).astype(jnp.bfloat16)
        mixed = lanes_to_rows(dot(parts, wm[item]))
        square = dot(yt[item], jnp.concatenate(halves(mixed), axis=1))
        square = jnp.where(block_mask, join_lanes(join_rows(square)), 0.0)
        total = square[:chi]
        for i in range(1, rep):
            total = total + square[i * chi : (i + 1) * chi]
        return normalize(fold(total))

    envs = [[unflatten(leaf_ref[0, n : n + 1, :]) for n in range(leaves)]]
    advance()
    for copy in local_moves[0]:
        copy.wait_recv()
    waited = 1
    node = 0
    for height in range(1, height_dev + 1):
        if height == 2:
            for copy in local_moves[1]:
                copy.wait_recv()
        current = envs[-1]
        grown = []
        for n in range(leaves >> height):
            value = jnp.concatenate([loc[j, node] for j in range(bonds)], axis=0)
            store(2 * node, value)
            store(2 * node + 1, swap_children(value))
            left, right = current[2 * n], current[2 * n + 1]
            by_left = act_major(2 * node, left)
            act_major(2 * node + 1, right)
            grown.append(close(by_left, act_minor(2 * node, right)))
            node += 1
            advance()
        envs.append(grown)
    while len(forward_moves) < levels:
        advance()

    env = envs[-1][0]

    def assemble(k, start, width):
        count = min(2 << k, devices)
        base = (position >> (k + 1)) << (k + 1)
        rows = []
        for j in range(bonds):
            rows.append(
                jnp.concatenate(
                    [raw[j, base + s, :, start : start + width] for s in range(count)], axis=1
                )
            )
        return jnp.concatenate(rows, axis=0)

    exchanges = []
    for k in range(levels):
        esend[k] = env
        copy = pltpu.make_async_remote_copy(
            src_ref=esend.at[k],
            dst_ref=erecv.at[k],
            send_sem=env_send.at[k],
            recv_sem=env_recv.at[k],
            device_id=(leaf_peers[k], mine),
            device_id_type=MESH,
        )
        copy.start()
        sends.append(copy)
        for move in forward_moves[k]:
            move.wait_recv()
        item = 2 * nodes + k
        value = assemble(k, starts[k], cols >> (k + 1))
        upper = lax.rem(position >> k, 2) == 1
        store(item, jnp.where(upper, value, swap_children(value)))
        minor = act_minor(item, env)
        copy.wait_recv()
        env = close(act_major(item, erecv[k]), minor)

    root = assemble(levels - 1, starts[levels], cols >> levels)
    state = close(root, root)
    top = env
    for k in range(levels - 1, -1, -1):
        marked = lax.rem(position + 1, 2 << k) == 1 << k
        top = jnp.where(marked, state, top)
        state = descend(2 * nodes + k, state)
    flatten(top, top_out, 0)
    states = [state]
    for height in range(height_dev, 0, -1):
        count = leaves >> height
        offset = leaves - 2 * count
        below = []
        for n in range(count):
            node = offset + n
            flatten(states[n], inner_out, node)
            below.append(descend(2 * node + 1, states[n]))
            below.append(descend(2 * node, states[n]))
        states = below
    for n in range(leaves):
        flatten(states[n], leaf_out, n)
    for copy in sends:
        copy.wait_send()


def body(cfg, leaf_metric, local_iso, top_iso):
    chi, leaves, devices, bonds = cfg
    cols = chi * chi
    nodes = leaves - 1
    levels = devices.bit_length() - 1
    share = chi // bonds
    items = 2 * nodes + levels
    f32 = jnp.float32
    dma = pltpu.SemaphoreType.DMA
    vmem = pl.BlockSpec(memory_space=pltpu.VMEM)
    return pl.pallas_call(
        functools.partial(kernel, cfg),
        out_shape=(
            jax.ShapeDtypeStruct((1, leaves, cols), f32),
            jax.ShapeDtypeStruct((1, nodes, cols), f32),
            jax.ShapeDtypeStruct((1, 1, cols), f32),
        ),
        in_specs=[vmem] * 3,
        out_specs=(vmem,) * 3,
        scratch_shapes=[
            pltpu.VMEM((bonds, devices, share, cols), f32),
            pltpu.VMEM((bonds, nodes, share, cols), f32),
            pltpu.VMEM((items, cols * chi // LANES, 2 * LANES), jnp.bfloat16),
            pltpu.VMEM((items, LANES, cols), jnp.bfloat16),
            pltpu.VMEM((items, cols * chi // LANES, 2 * LANES), jnp.bfloat16),
            pltpu.VMEM((items, 2 * LANES, cols * chi // LANES), jnp.bfloat16),
            pltpu.VMEM((chi, cols * chi // LANES), f32),
            pltpu.VMEM((cols, chi), f32),
            pltpu.VMEM((levels, chi, LANES), f32),
            pltpu.VMEM((levels, chi, LANES), f32),
            dma((2,)),
            dma((2, bonds - 1)),
            dma((2, bonds - 1)),
            dma((levels,)),
            dma((levels,)),
            dma((levels, bonds - 1)),
            dma((levels, bonds - 1)),
            dma((levels,)),
            dma((levels,)),
        ],
        compiler_params=pltpu.CompilerParams(collective_id=0, has_side_effects=True),
        name="tree_sweep",
    )(leaf_metric, local_iso, top_iso)


def solution(mesh):
    devices, bonds = mesh.shape["leaf"], mesh.shape["bond"]
    spec = P("bond", "leaf", None)
    iso = P("leaf", "bond", None)

    def whole(leaf_metric, local_iso, top_iso):
        cfg = (local_iso.shape[1], leaf_metric.shape[1] // devices, devices, bonds)
        return jax.shard_map(
            functools.partial(body, cfg),
            mesh=mesh,
            in_specs=(spec, iso, iso),
            out_specs=(spec, spec, spec),
            check_vma=False,
        )(leaf_metric, local_iso, top_iso)

    return whole
```

```python
import functools

import jax
import jax.numpy as jnp
from jax import lax
from jax.experimental import pallas as pl
from jax.experimental.pallas import tpu as pltpu
from jax.sharding import PartitionSpec as P

LANES = 128
MESH = pl.DeviceIdType.MESH
EXACT = lax.Precision.HIGHEST


def mm(a, b):
    return jnp.dot(a, b, precision=EXACT, preferred_element_type=jnp.float32)


def dot(a, b):
    return jnp.dot(a, b, preferred_element_type=jnp.float32)


def dot_nt(a, b):
    return lax.dot_general(a, b, (((1,), (1,)), ((), ())), preferred_element_type=jnp.float32)


def halves(value):
    high = value.astype(jnp.bfloat16)
    low = (value - high.astype(jnp.float32)).astype(jnp.bfloat16)
    return high, low


def join_lanes(value):
    return value[:, :LANES] + value[:, LANES:]


def join_rows(value):
    half = value.shape[0] // 2
    return value[:half] + value[half:]


def kernel(
    cfg,
    leaf_ref,
    local_ref,
    top_ref,
    leaf_out,
    inner_out,
    top_out,
    raw,
    loc,
    wk,
    wm,
    wq,
    yt,
    fbuf,
    tbuf,
    esend,
    erecv,
    own_sem,
    loc_send,
    loc_recv,
    leaf_send,
    leaf_recv,
    fwd_send,
    fwd_recv,
    env_send,
    env_recv,
):
    chi, leaves, devices, bonds = cfg
    cols = chi * chi
    rep = LANES // chi
    chunks = cols // LANES
    levels = devices.bit_length() - 1
    height_dev = leaves.bit_length() - 1
    nodes = leaves - 1
    first = leaves // 2
    position = lax.axis_index("leaf")
    mine = lax.axis_index("bond")

    leaf_peers = [position ^ (1 << k) for k in range(levels)]
    bond_peers = [lax.rem(mine + r, bonds) for r in range(1, bonds)]

    barrier = pltpu.get_barrier_semaphore()
    for peer in leaf_peers:
        pl.semaphore_signal(barrier, inc=1, device_id=(peer, mine), device_id_type=MESH)
    for peer in bond_peers:
        pl.semaphore_signal(barrier, inc=1, device_id=(position, peer), device_id_type=MESH)
    own = [
        pltpu.make_async_copy(top_ref.at[0], raw.at[mine, position], own_sem.at[0]),
        pltpu.make_async_copy(local_ref, loc.at[mine], own_sem.at[1]),
    ]
    for copy in own:
        copy.start()
    pl.semaphore_wait(barrier, levels + bonds - 1)

    starts = [cols - (cols >> k) for k in range(levels + 1)]
    aligned = [s // LANES * LANES for s in starts]
    sends = []

    def local_copies(part, lo, hi):
        found = []
        for r, peer in enumerate(bond_peers):
            found.append(
                pltpu.make_async_remote_copy(
                    src_ref=local_ref.at[lo:hi],
                    dst_ref=loc.at[mine, lo:hi],
                    send_sem=loc_send.at[part, r],
                    recv_sem=loc_recv.at[part, r],
                    device_id=(position, peer),
                    device_id_type=MESH,
                )
            )
        for copy in found:
            copy.start()
        sends.extend(found)
        return found

    def leaf_copy(k):
        base = (position >> k) << k
        slots = raw.at[mine, pl.ds(base, 1 << k), :, aligned[k] : cols]
        source = slots if k else top_ref
        copy = pltpu.make_async_remote_copy(
            src_ref=source,
            dst_ref=slots,
            send_sem=leaf_send.at[k],
            recv_sem=leaf_recv.at[k],
            device_id=(leaf_peers[k], mine),
            device_id_type=MESH,
        )
        copy.start()
        sends.append(copy)
        return copy

    def forward_copies(k):
        base = (position >> (k + 1)) << (k + 1)
        stop = cols if k == levels - 1 else -(-starts[k + 1] // LANES) * LANES
        found = []
        for r, peer in enumerate(bond_peers):
            slots = raw.at[mine, pl.ds(base, 2 << k), :, aligned[k] : stop]
            found.append(
                pltpu.make_async_remote_copy(
                    src_ref=slots,
                    dst_ref=slots,
                    send_sem=fwd_send.at[k, r],
                    recv_sem=fwd_recv.at[k, r],
                    device_id=(position, peer),
                    device_id_type=MESH,
                )
            )
        for copy in found:
            copy.start()
        sends.extend(found)
        return found

    local_moves = [local_copies(0, 0, first)]
    leaf_moves = [leaf_copy(0)]
    if nodes > first:
        local_moves.append(local_copies(1, first, nodes))
    forward_moves = []
    for copy in own:
        copy.wait()

    def advance():
        k = len(forward_moves)
        if k < levels:
            leaf_moves[k].wait_recv()
            if k + 1 < levels:
                leaf_moves.append(leaf_copy(k + 1))
            forward_moves.append(forward_copies(k))

    row = lax.broadcasted_iota(jnp.int32, (chi, LANES), 0)
    lane = lax.broadcasted_iota(jnp.int32, (chi, LANES), 1)
    group = lane // chi
    row_mask = group == lax.rem(row, rep)
    diag_mask = row == lane
    big_row = lax.broadcasted_iota(jnp.int32, (LANES, LANES), 0)
    big_lane = lax.broadcasted_iota(jnp.int32, (LANES, LANES), 1)
    block_mask = big_row // chi == big_lane // chi
    pick = (
        lax.broadcasted_iota(jnp.int32, (chunks, chi), 1) // rep
        == lax.broadcasted_iota(jnp.int32, (chunks, chi), 0)
    ).astype(jnp.float32)
    spread = (
        lax.broadcasted_iota(jnp.int32, (chi, chunks), 0) // rep
        == lax.broadcasted_iota(jnp.int32, (chi, chunks), 1)
    ).astype(jnp.float32)
    sub = chi // rep
    widen = (
        lax.broadcasted_iota(jnp.int32, (LANES, chi * sub), 1) // sub
        == lax.rem(lax.broadcasted_iota(jnp.int32, (LANES, chi * sub), 0), chi)
    ).astype(jnp.float32).astype(jnp.bfloat16)
    unit_mask = lax.rem(
        lax.broadcasted_iota(jnp.int32, (sub, chi * sub), 1), sub
    ) == lax.broadcasted_iota(jnp.int32, (sub, chi * sub), 0)
    part_group = lax.broadcasted_iota(jnp.int32, (chunks * sub, LANES), 1) // chi

    def swap_groups(value):
        parts = [
            jnp.concatenate(
                [value[g * chi + v * sub : g * chi + (v + 1) * sub] for g in range(chunks)], axis=0
            )
            for v in range(rep)
        ]
        bit = 1
        while bit < rep:
            lower = lax.rem(part_group // bit, 2) == 0
            for a in range(rep):
                if a & bit == 0:
                    one, two = parts[a], parts[a | bit]
                    parts[a] = jnp.where(lower, one, pltpu.roll(two, bit * chi, 1))
                    parts[a | bit] = jnp.where(lower, pltpu.roll(one, LANES - bit * chi, 1), two)
            bit *= 2
        return jnp.concatenate(
            [parts[v][g * sub : (g + 1) * sub] for g in range(chunks) for v in range(rep)], axis=0
        )

    def fold(value):
        shift = chi
        while shift < LANES:
            value = value + pltpu.roll(value, shift, 1)
            shift *= 2
        return value

    def normalize(matrix):
        trace = jnp.sum(jnp.where(diag_mask, matrix, 0.0), axis=(0, 1), keepdims=True)
        return matrix * (chi / trace)

    def unflatten(line):
        tile = jnp.concatenate(
            [line[:, g * LANES : (g + 1) * LANES] for g in range(chunks)], axis=0
        )
        return fold(jnp.where(row_mask, mm(spread, tile), 0.0))

    def flatten(matrix, out, index, lead=0):
        tile = mm(pick, jnp.where(row_mask, matrix, 0.0))
        for g in range(chunks):
            out[lead, index : index + 1, g * LANES : (g + 1) * LANES] = tile[g : g + 1]

    def lanes_to_rows(value):
        return jnp.concatenate(
            [value[:, g * LANES : (g + 1) * LANES] for g in range(chunks)], axis=0
        )

    def rows_to_lanes(value):
        return jnp.concatenate([value[g * chi : (g + 1) * chi] for g in range(chunks)], axis=1)

    def swap_children(value):
        for g in range(chunks):
            tbuf[g * LANES : (g + 1) * LANES, :] = value[:, g * LANES : (g + 1) * LANES].T
        pieces = []
        for g in range(chunks):
            block = jnp.concatenate(
                [tbuf[pl.ds(rep * g + i, chi, stride=chi), :] for i in range(rep)], axis=0
            )
            pieces.append(block.T)
        return jnp.concatenate(pieces, axis=1)

    def store(item, value):
        high, low = halves(value)
        wm[item] = jnp.concatenate([high, low] * (rep // 2), axis=0)
        stack = jnp.concatenate([lanes_to_rows(high), lanes_to_rows(low)], axis=1)
        wk[item] = stack
        wq[item] = jnp.concatenate(halves(swap_groups(lanes_to_rows(value))), axis=1)

    def act_minor(item, env):
        block = jnp.where(block_mask, jnp.concatenate([env] * rep, axis=0), 0.0)
        pair = jnp.concatenate(halves(block), axis=1)
        return rows_to_lanes(join_lanes(dot(wk[item], jnp.concatenate([pair, pair], axis=0))))

    def act_major(item, env):
        high = env.astype(jnp.bfloat16).astype(jnp.float32)
        rest = env - high
        middle = rest.astype(jnp.bfloat16).astype(jnp.float32)
        low = jnp.where(group == 2, rest - middle, 0.0)
        parts = jnp.where(group == 0, high, jnp.where(group == 1, middle, low))
        fbuf[...] = dot(parts.astype(jnp.bfloat16), widen)
        wide = jnp.concatenate(
            [
                jnp.where(unit_mask, jnp.broadcast_to(fbuf[y : y + 1, :], unit_mask.shape), 0.0)
                for y in range(chi)
            ],
            axis=0,
        )
        acted = dot(jnp.concatenate(halves(wide), axis=0), wq[item])
        acted = swap_groups(join_lanes(join_rows(acted)))
        yt[item] = jnp.concatenate(halves(acted.T), axis=0)
        return rows_to_lanes(acted)

    def close(left, right):
        high, low = halves(right)
        wide = jnp.concatenate([high] * rep + [low] * rep, axis=0)
        tall = jnp.concatenate(halves(left), axis=0)
        return normalize(join_lanes(join_rows(dot_nt(tall, wide))))

    def descend(item, state):
        high = state.astype(jnp.bfloat16).astype(jnp.float32)
        parts = jnp.where(group < rep // 2, high, state - high).astype(jnp.bfloat16)
        mixed = lanes_to_rows(dot(parts, wm[item]))
        square = dot(yt[item], jnp.concatenate(halves(mixed), axis=1))
        square = jnp.where(block_mask, join_lanes(join_rows(square)), 0.0)
        total = square[:chi]
        for i in range(1, rep):
            total = total + square[i * chi : (i + 1) * chi]
        return normalize(fold(total))

    envs = [[unflatten(leaf_ref[0, n : n + 1, :]) for n in range(leaves)]]
    advance()
    for copy in local_moves[0]:
        copy.wait_recv()
    node = 0
    late = []
    for height in range(1, height_dev + 1):
        if height == 2:
            for copy in local_moves[1]:
                copy.wait_recv()
        current = envs[-1]
        grown = []
        for n in range(leaves >> height):
            value = jnp.concatenate([loc[j, node] for j in range(bonds)], axis=0)
            store(2 * node, value)
            left, right = current[2 * n], current[2 * n + 1]
            by_left = act_major(2 * node, left)
            late.append((node, right))
            grown.append(close(by_left, act_minor(2 * node, right)))
            node += 1
            advance()
        envs.append(grown)
    while len(forward_moves) < levels:
        advance()

    env = envs[-1][0]

    def assemble(k, start, width):
        count = min(2 << k, devices)
        base = (position >> (k + 1)) << (k + 1)
        rows = []
        for j in range(bonds):
            rows.append(
                jnp.concatenate(
                    [raw[j, base + s, :, start : start + width] for s in range(count)], axis=1
                )
            )
        return jnp.concatenate(rows, axis=0)

    exchanges = []
    for k in range(levels):
        esend[k] = env
        copy = pltpu.make_async_remote_copy(
            src_ref=esend.at[k],
            dst_ref=erecv.at[k],
            send_sem=env_send.at[k],
            recv_sem=env_recv.at[k],
            device_id=(leaf_peers[k], mine),
            device_id_type=MESH,
        )
        copy.start()
        sends.append(copy)
        for move in forward_moves[k]:
            move.wait_recv()
        item = 2 * nodes + k
        value = assemble(k, starts[k], cols >> (k + 1))
        upper = lax.rem(position >> k, 2) == 1
        store(item, jnp.where(upper, value, swap_children(value)))
        minor = act_minor(item, env)
        if k == levels - 1:
            root = assemble(levels - 1, starts[levels], cols >> levels)
            state = close(root, root)
        for other, right in late[k::levels]:
            value = jnp.concatenate([loc[j, other] for j in range(bonds)], axis=0)
            store(2 * other + 1, swap_children(value))
            act_major(2 * other + 1, right)
        copy.wait_recv()
        env = close(act_major(item, erecv[k]), minor)

    top = env
    for k in range(levels - 1, -1, -1):
        marked = lax.rem(position + 1, 2 << k) == 1 << k
        top = jnp.where(marked, state, top)
        state = descend(2 * nodes + k, state)
    flatten(top, top_out, 0)
    states = [state]
    for height in range(height_dev, 0, -1):
        count = leaves >> height
        offset = leaves - 2 * count
        below = []
        for n in range(count):
            node = offset + n
            flatten(states[n], inner_out, 0, node)
            below.append(descend(2 * node + 1, states[n]))
            below.append(descend(2 * node, states[n]))
        states = below
    for n in range(leaves):
        flatten(states[n], leaf_out, n)
    for copy in sends:
        copy.wait_send()


def body(cfg, leaf_metric, local_iso, top_iso):
    chi, leaves, devices, bonds = cfg
    cols = chi * chi
    nodes = leaves - 1
    levels = devices.bit_length() - 1
    share = chi // bonds
    items = 2 * nodes + levels
    f32 = jnp.float32
    dma = pltpu.SemaphoreType.DMA
    vmem = pl.BlockSpec(memory_space=pltpu.VMEM)
    leaf_rho, inner_rho, top_rho = pl.pallas_call(
        functools.partial(kernel, cfg),
        out_shape=(
            jax.ShapeDtypeStruct((1, leaves, cols), f32),
            jax.ShapeDtypeStruct((nodes, 1, cols), f32),
            jax.ShapeDtypeStruct((1, 1, cols), f32),
        ),
        in_specs=[vmem] * 3,
        out_specs=(vmem,) * 3,
        scratch_shapes=[
            pltpu.VMEM((bonds, devices, share, cols), f32),
            pltpu.VMEM((bonds, nodes, share, cols), f32),
            pltpu.VMEM((items, cols * chi // LANES, 2 * LANES), jnp.bfloat16),
            pltpu.VMEM((items, LANES, cols), jnp.bfloat16),
            pltpu.VMEM((items, cols * chi // LANES, 2 * LANES), jnp.bfloat16),
            pltpu.VMEM((items, 2 * LANES, cols * chi // LANES), jnp.bfloat16),
            pltpu.VMEM((chi, cols * chi // LANES), f32),
            pltpu.VMEM((cols, chi), f32),
            pltpu.VMEM((levels, chi, LANES), f32),
            pltpu.VMEM((levels, chi, LANES), f32),
            dma((2,)),
            dma((2, bonds - 1)),
            dma((2, bonds - 1)),
            dma((levels,)),
            dma((levels,)),
            dma((levels, bonds - 1)),
            dma((levels, bonds - 1)),
            dma((levels,)),
            dma((levels,)),
        ],
        compiler_params=pltpu.CompilerParams(collective_id=0, has_side_effects=True),
        name="tree_sweep",
    )(leaf_metric, local_iso, top_iso)
    return leaf_rho, inner_rho.transpose(1, 0, 2), top_rho


def solution(mesh):
    devices, bonds = mesh.shape["leaf"], mesh.shape["bond"]
    spec = P("bond", "leaf", None)
    iso = P("leaf", "bond", None)

    def whole(leaf_metric, local_iso, top_iso):
        cfg = (local_iso.shape[1], leaf_metric.shape[1] // devices, devices, bonds)
        return jax.shard_map(
            functools.partial(body, cfg),
            mesh=mesh,
            in_specs=(spec, iso, iso),
            out_specs=(spec, spec, spec),
            check_vma=False,
        )(leaf_metric, local_iso, top_iso)

    return whole
```

```python
import functools

import jax
import jax.numpy as jnp
from jax import lax
from jax.experimental import pallas as pl
from jax.experimental.pallas import tpu as pltpu
from jax.sharding import PartitionSpec as P

LANES = 128
MESH = pl.DeviceIdType.MESH
EXACT = lax.Precision.HIGHEST


def mm(a, b):
    return jnp.dot(a, b, precision=EXACT, preferred_element_type=jnp.float32)


def dot(a, b):
    return jnp.dot(a, b, preferred_element_type=jnp.float32)


def dot_nt(a, b):
    return lax.dot_general(a, b, (((1,), (1,)), ((), ())), preferred_element_type=jnp.float32)


def halves(value):
    high = value.astype(jnp.bfloat16)
    low = (value - high.astype(jnp.float32)).astype(jnp.bfloat16)
    return high, low


def join_lanes(value):
    return value[:, :LANES] + value[:, LANES:]


def join_rows(value):
    half = value.shape[0] // 2
    return value[:half] + value[half:]


def kernel(
    cfg,
    leaf_ref,
    local_ref,
    top_ref,
    leaf_out,
    inner_out,
    top_out,
    raw,
    loc,
    wk,
    wm,
    wq,
    yt,
    fbuf,
    tbuf,
    esend,
    erecv,
    own_sem,
    loc_send,
    loc_recv,
    leaf_send,
    leaf_recv,
    fwd_send,
    fwd_recv,
    env_send,
    env_recv,
):
    chi, leaves, devices, bonds = cfg
    cols = chi * chi
    rep = LANES // chi
    chunks = cols // LANES
    levels = devices.bit_length() - 1
    height_dev = leaves.bit_length() - 1
    nodes = leaves - 1
    position = lax.axis_index("leaf")
    mine = lax.axis_index("bond")

    leaf_peers = [position ^ (1 << k) for k in range(levels)]
    bond_peers = [lax.rem(mine + r, bonds) for r in range(1, bonds)]

    barrier = pltpu.get_barrier_semaphore()
    for peer in leaf_peers:
        pl.semaphore_signal(barrier, inc=1, device_id=(peer, mine), device_id_type=MESH)
    for peer in bond_peers:
        pl.semaphore_signal(barrier, inc=1, device_id=(position, peer), device_id_type=MESH)
    own = [
        pltpu.make_async_copy(top_ref.at[0], raw.at[mine, position], own_sem.at[0]),
        pltpu.make_async_copy(local_ref, loc.at[mine], own_sem.at[1]),
    ]
    for copy in own:
        copy.start()
    pl.semaphore_wait(barrier, levels + bonds - 1)

    starts = [cols - (cols >> k) for k in range(levels + 1)]
    aligned = [s // LANES * LANES for s in starts]
    sends = []

    def local_copies(part, lo, hi):
        found = []
        for r, peer in enumerate(bond_peers):
            found.append(
                pltpu.make_async_remote_copy(
                    src_ref=local_ref.at[lo:hi],
                    dst_ref=loc.at[mine, lo:hi],
                    send_sem=loc_send.at[part, r],
                    recv_sem=loc_recv.at[part, r],
                    device_id=(position, peer),
                    device_id_type=MESH,
                )
            )
        for copy in found:
            copy.start()
        sends.extend(found)
        return found

    def leaf_copy(k):
        base = (position >> k) << k
        slots = raw.at[mine, pl.ds(base, 1 << k), :, aligned[k] : cols]
        source = slots if k else top_ref
        copy = pltpu.make_async_remote_copy(
            src_ref=source,
            dst_ref=slots,
            send_sem=leaf_send.at[k],
            recv_sem=leaf_recv.at[k],
            device_id=(leaf_peers[k], mine),
            device_id_type=MESH,
        )
        copy.start()
        sends.append(copy)
        return copy

    def forward_copies(k):
        base = (position >> (k + 1)) << (k + 1)
        stop = cols if k == levels - 1 else -(-starts[k + 1] // LANES) * LANES
        found = []
        for r, peer in enumerate(bond_peers):
            slots = raw.at[mine, pl.ds(base, 2 << k), :, aligned[k] : stop]
            found.append(
                pltpu.make_async_remote_copy(
                    src_ref=slots,
                    dst_ref=slots,
                    send_sem=fwd_send.at[k, r],
                    recv_sem=fwd_recv.at[k, r],
                    device_id=(position, peer),
                    device_id_type=MESH,
                )
            )
        for copy in found:
            copy.start()
        sends.extend(found)
        return found

    local_moves = [local_copies(0, 0, 1)]
    leaf_moves = [leaf_copy(0)]
    for n in range(1, nodes):
        local_moves.append(local_copies(n, n, n + 1))
    forward_moves = []
    for copy in own:
        copy.wait()

    def advance():
        k = len(forward_moves)
        if k < levels:
            leaf_moves[k].wait_recv()
            if k + 1 < levels:
                leaf_moves.append(leaf_copy(k + 1))
            forward_moves.append(forward_copies(k))

    row = lax.broadcasted_iota(jnp.int32, (chi, LANES), 0)
    lane = lax.broadcasted_iota(jnp.int32, (chi, LANES), 1)
    group = lane // chi
    row_mask = group == lax.rem(row, rep)
    diag_mask = row == lane
    big_row = lax.broadcasted_iota(jnp.int32, (LANES, LANES), 0)
    big_lane = lax.broadcasted_iota(jnp.int32, (LANES, LANES), 1)
    block_mask = big_row // chi == big_lane // chi
    pick = (
        lax.broadcasted_iota(jnp.int32, (chunks, chi), 1) // rep
        == lax.broadcasted_iota(jnp.int32, (chunks, chi), 0)
    ).astype(jnp.float32)
    spread = (
        lax.broadcasted_iota(jnp.int32, (chi, chunks), 0) // rep
        == lax.broadcasted_iota(jnp.int32, (chi, chunks), 1)
    ).astype(jnp.float32)
    sub = chi // rep
    widen = (
        lax.broadcasted_iota(jnp.int32, (LANES, chi * sub), 1) // sub
        == lax.rem(lax.broadcasted_iota(jnp.int32, (LANES, chi * sub), 0), chi)
    ).astype(jnp.float32).astype(jnp.bfloat16)
    unit_mask = lax.rem(
        lax.broadcasted_iota(jnp.int32, (sub, chi * sub), 1), sub
    ) == lax.broadcasted_iota(jnp.int32, (sub, chi * sub), 0)
    part_group = lax.broadcasted_iota(jnp.int32, (chunks * sub, LANES), 1) // chi

    def swap_groups(value):
        parts = [
            jnp.concatenate(
                [value[g * chi + v * sub : g * chi + (v + 1) * sub] for g in range(chunks)], axis=0
            )
            for v in range(rep)
        ]
        bit = 1
        while bit < rep:
            lower = lax.rem(part_group // bit, 2) == 0
            for a in range(rep):
                if a & bit == 0:
                    one, two = parts[a], parts[a | bit]
                    parts[a] = jnp.where(lower, one, pltpu.roll(two, bit * chi, 1))
                    parts[a | bit] = jnp.where(lower, pltpu.roll(one, LANES - bit * chi, 1), two)
            bit *= 2
        return jnp.concatenate(
            [parts[v][g * sub : (g + 1) * sub] for g in range(chunks) for v in range(rep)], axis=0
        )

    def fold(value):
        shift = chi
        while shift < LANES:
            value = value + pltpu.roll(value, shift, 1)
            shift *= 2
        return value

    def normalize(matrix):
        trace = jnp.sum(jnp.where(diag_mask, matrix, 0.0), axis=(0, 1), keepdims=True)
        return matrix * (chi / trace)

    def unflatten(line):
        tile = jnp.concatenate(
            [line[:, g * LANES : (g + 1) * LANES] for g in range(chunks)], axis=0
        )
        return fold(jnp.where(row_mask, mm(spread, tile), 0.0))

    def flatten(matrix, out, index, lead=0):
        tile = mm(pick, jnp.where(row_mask, matrix, 0.0))
        for g in range(chunks):
            out[lead, index : index + 1, g * LANES : (g + 1) * LANES] = tile[g : g + 1]

    def lanes_to_rows(value):
        return jnp.concatenate(
            [value[:, g * LANES : (g + 1) * LANES] for g in range(chunks)], axis=0
        )

    def rows_to_lanes(value):
        return jnp.concatenate([value[g * chi : (g + 1) * chi] for g in range(chunks)], axis=1)

    def swap_children(value):
        for g in range(chunks):
            tbuf[g * LANES : (g + 1) * LANES, :] = value[:, g * LANES : (g + 1) * LANES].T
        pieces = []
        for g in range(chunks):
            block = jnp.concatenate(
                [tbuf[pl.ds(rep * g + i, chi, stride=chi), :] for i in range(rep)], axis=0
            )
            pieces.append(block.T)
        return jnp.concatenate(pieces, axis=1)

    def store(item, value):
        high, low = halves(value)
        wm[item] = jnp.concatenate([high, low] * (rep // 2), axis=0)
        stack = jnp.concatenate([lanes_to_rows(high), lanes_to_rows(low)], axis=1)
        wk[item] = stack
        wq[item] = jnp.concatenate(halves(swap_groups(lanes_to_rows(value))), axis=1)

    def act_minor(item, env):
        block = jnp.where(block_mask, jnp.concatenate([env] * rep, axis=0), 0.0)
        pair = jnp.concatenate(halves(block), axis=1)
        return rows_to_lanes(join_lanes(dot(wk[item], jnp.concatenate([pair, pair], axis=0))))

    def act_major(item, env):
        high = env.astype(jnp.bfloat16).astype(jnp.float32)
        rest = env - high
        middle = rest.astype(jnp.bfloat16).astype(jnp.float32)
        low = jnp.where(group == 2, rest - middle, 0.0)
        parts = jnp.where(group == 0, high, jnp.where(group == 1, middle, low))
        fbuf[...] = dot(parts.astype(jnp.bfloat16), widen)
        wide = jnp.concatenate(
            [
                jnp.where(unit_mask, jnp.broadcast_to(fbuf[y : y + 1, :], unit_mask.shape), 0.0)
                for y in range(chi)
            ],
            axis=0,
        )
        acted = dot(jnp.concatenate(halves(wide), axis=0), wq[item])
        acted = swap_groups(join_lanes(join_rows(acted)))
        yt[item] = jnp.concatenate(halves(acted.T), axis=0)
        return rows_to_lanes(acted)

    def close(left, right):
        high, low = halves(right)
        wide = jnp.concatenate([high] * rep + [low] * rep, axis=0)
        tall = jnp.concatenate(halves(left), axis=0)
        return normalize(join_lanes(join_rows(dot_nt(tall, wide))))

    def descend(item, state):
        high = state.astype(jnp.bfloat16).astype(jnp.float32)
        parts = jnp.where(group < rep // 2, high, state - high).astype(jnp.bfloat16)
        mixed = lanes_to_rows(dot(parts, wm[item]))
        square = dot(yt[item], jnp.concatenate(halves(mixed), axis=1))
        square = jnp.where(block_mask, join_lanes(join_rows(square)), 0.0)
        total = square[:chi]
        for i in range(1, rep):
            total = total + square[i * chi : (i + 1) * chi]
        return normalize(fold(total))

    envs = [[unflatten(leaf_ref[0, n : n + 1, :]) for n in range(leaves)]]
    advance()
    node = 0
    late = []
    for height in range(1, height_dev + 1):
        current = envs[-1]
        grown = []
        for n in range(leaves >> height):
            for copy in local_moves[node]:
                copy.wait_recv()
            value = jnp.concatenate([loc[j, node] for j in range(bonds)], axis=0)
            store(2 * node, value)
            left, right = current[2 * n], current[2 * n + 1]
            by_left = act_major(2 * node, left)
            late.append((node, right))
            grown.append(close(by_left, act_minor(2 * node, right)))
            node += 1
            advance()
        envs.append(grown)
    while len(forward_moves) < levels:
        advance()

    env = envs[-1][0]

    def assemble(k, start, width):
        count = min(2 << k, devices)
        base = (position >> (k + 1)) << (k + 1)
        rows = []
        for j in range(bonds):
            rows.append(
                jnp.concatenate(
                    [raw[j, base + s, :, start : start + width] for s in range(count)], axis=1
                )
            )
        return jnp.concatenate(rows, axis=0)

    exchanges = []
    for k in range(levels):
        esend[k] = env
        copy = pltpu.make_async_remote_copy(
            src_ref=esend.at[k],
            dst_ref=erecv.at[k],
            send_sem=env_send.at[k],
            recv_sem=env_recv.at[k],
            device_id=(leaf_peers[k], mine),
            device_id_type=MESH,
        )
        copy.start()
        sends.append(copy)
        for move in forward_moves[k]:
            move.wait_recv()
        item = 2 * nodes + k
        value = assemble(k, starts[k], cols >> (k + 1))
        upper = lax.rem(position >> k, 2) == 1
        store(item, jnp.where(upper, value, swap_children(value)))
        minor = act_minor(item, env)
        if k == levels - 1:
            root = assemble(levels - 1, starts[levels], cols >> levels)
            state = close(root, root)
        for other, right in late[k::levels]:
            value = jnp.concatenate([loc[j, other] for j in range(bonds)], axis=0)
            store(2 * other + 1, swap_children(value))
            act_major(2 * other + 1, right)
        copy.wait_recv()
        env = close(act_major(item, erecv[k]), minor)

    top = env
    for k in range(levels - 1, -1, -1):
        marked = lax.rem(position + 1, 2 << k) == 1 << k
        top = jnp.where(marked, state, top)
        state = descend(2 * nodes + k, state)
    flatten(top, top_out, 0)
    states = [state]
    for height in range(height_dev, 0, -1):
        count = leaves >> height
        offset = leaves - 2 * count
        below = []
        for n in range(count):
            node = offset + n
            flatten(states[n], inner_out, 0, node)
            below.append(descend(2 * node + 1, states[n]))
            below.append(descend(2 * node, states[n]))
        states = below
    for n in range(leaves):
        flatten(states[n], leaf_out, n)
    for copy in sends:
        copy.wait_send()


def body(cfg, leaf_metric, local_iso, top_iso):
    chi, leaves, devices, bonds = cfg
    cols = chi * chi
    nodes = leaves - 1
    levels = devices.bit_length() - 1
    share = chi // bonds
    items = 2 * nodes + levels
    f32 = jnp.float32
    dma = pltpu.SemaphoreType.DMA
    vmem = pl.BlockSpec(memory_space=pltpu.VMEM)
    leaf_rho, inner_rho, top_rho = pl.pallas_call(
        functools.partial(kernel, cfg),
        out_shape=(
            jax.ShapeDtypeStruct((1, leaves, cols), f32),
            jax.ShapeDtypeStruct((nodes, 1, cols), f32),
            jax.ShapeDtypeStruct((1, 1, cols), f32),
        ),
        in_specs=[vmem] * 3,
        out_specs=(vmem,) * 3,
        scratch_shapes=[
            pltpu.VMEM((bonds, devices, share, cols), f32),
            pltpu.VMEM((bonds, nodes, share, cols), f32),
            pltpu.VMEM((items, cols * chi // LANES, 2 * LANES), jnp.bfloat16),
            pltpu.VMEM((items, LANES, cols), jnp.bfloat16),
            pltpu.VMEM((items, cols * chi // LANES, 2 * LANES), jnp.bfloat16),
            pltpu.VMEM((items, 2 * LANES, cols * chi // LANES), jnp.bfloat16),
            pltpu.VMEM((chi, cols * chi // LANES), f32),
            pltpu.VMEM((cols, chi), f32),
            pltpu.VMEM((levels, chi, LANES), f32),
            pltpu.VMEM((levels, chi, LANES), f32),
            dma((2,)),
            dma((nodes, bonds - 1)),
            dma((nodes, bonds - 1)),
            dma((levels,)),
            dma((levels,)),
            dma((levels, bonds - 1)),
            dma((levels, bonds - 1)),
            dma((levels,)),
            dma((levels,)),
        ],
        compiler_params=pltpu.CompilerParams(collective_id=0, has_side_effects=True),
        name="tree_sweep",
    )(leaf_metric, local_iso, top_iso)
    return leaf_rho, inner_rho.transpose(1, 0, 2), top_rho


def solution(mesh):
    devices, bonds = mesh.shape["leaf"], mesh.shape["bond"]
    spec = P("bond", "leaf", None)
    iso = P("leaf", "bond", None)

    def whole(leaf_metric, local_iso, top_iso):
        cfg = (local_iso.shape[1], leaf_metric.shape[1] // devices, devices, bonds)
        return jax.shard_map(
            functools.partial(body, cfg),
            mesh=mesh,
            in_specs=(spec, iso, iso),
            out_specs=(spec, spec, spec),
            check_vma=False,
        )(leaf_metric, local_iso, top_iso)

    return whole
```
